256 devices in a mesh: row: 8 (over z), col: 32 (over y, x, core).
Axes of the slice: x: 4, y: 4, z: 8, core: 2. Of those that a mesh axis runs over, the one named last changes fastest.
Arguments:
- sources: float32 [30, 32768], P(None, ('row', 'col')), may hold values from -12 to 12
- log_source_mass: float32 [32768], P(('row', 'col')), may hold values from -4 to 4
- targets: float32 [30, 16384], P(None, 'col'), may hold values from -6 to 6
- log_target_mass: float32 [16384], P('col'), may hold values from -4 to 4
- start_potential: float32 [16384], P('col'), may hold values from -12 to 250
Outputs:
- row_potential: float32 [32768], P(('row', 'col'))
- column_potential: float32 [16384], P('col')
The draws below stay inside these ranges and needn't reach their ends.
All inputs are finite; a program needn't handle non-finite values.
Results may differ from the reference program's by a relative error of at most 0.00015.
Values sent between devices are 32-bit elements; how exact they have to be, the bound alone decides.
No kernel may reach another device: no remote copies, remote signals or barrier semaphores. Data moves between devices by JAX's collectives and lax.ppermute only.
A program may use at most 64 MiB of HBM per device.

```python
import jax
import jax.numpy as jnp
from jax import lax

D = 30
ITERS = 2
SRC = 32768
TGT = 16384


def draw_sources(key, part):
    base = jax.random.normal(jax.random.fold_in(key, 11), (D, SRC), jnp.float32)
    return jnp.clip(base, -12.0, 12.0)


def draw_start_potential(key, part):
    base = 2.0 * jax.random.normal(jax.random.fold_in(key, 21), (TGT,), jnp.float32)
    return jnp.clip(base, -12.0, 250.0)


def levels(stream_key, extent, pieces, least, largest):
    factor_of, own = 1.0, jax.random.fold_in(stream_key, 6)
    for axis_at, parts in pieces:
        steps = jnp.exp(jax.random.uniform(jax.random.fold_in(own, axis_at), (parts,), jnp.float32, least / len(pieces), largest / len(pieces)))
        factor_of = factor_of * jnp.repeat(steps, extent[axis_at] // parts).reshape([-1 if axis == axis_at else 1 for axis in range(len(extent))])
    return factor_of


def scatter_about(stream_key, extent, width, most, cuts=(), dtype=jnp.bfloat16):
    result = jax.random.normal(stream_key, extent, jnp.float32) * width
    if len(cuts) > 0:
        result = levels(stream_key, extent, cuts, -0.22, 0.18) * result
    return jnp.clip(result, min=-most, max=most).astype(dtype)


def setup_inputs(seed: int = 0) -> dict:
    splits = jax.random.split(jax.random.key(seed), 6)
    return {
        "sources": draw_sources(jax.random.fold_in(splits[5], 71), 0),
        "log_source_mass": scatter_about(splits[1], (SRC,), 1.0, 4.0, ((0, 256),), jnp.float32),
        "targets": scatter_about(splits[2], (D, TGT), 1.0, 6.0, ((1, 32),), jnp.float32),
        "log_target_mass": scatter_about(splits[3], (TGT,), 1.0, 4.0, ((0, 32),), jnp.float32),
        "start_potential": draw_start_potential(jax.random.fold_in(splits[5], 71), 0),
    }


entropic_scale = 2.0


def row_sweep(sources, targets, target_term):
    dims, count = sources.shape
    block_rows = 256 if count % 256 == 0 else count
    target_sq = 0.5 * jnp.sum(targets * targets, axis=0)
    blocks = sources.T.reshape(count // block_rows, block_rows, dims)

    def one_block(coords):
        inner = jnp.dot(coords, targets, precision=lax.Precision.HIGHEST, preferred_element_type=jnp.float32)
        cost = 0.5 * jnp.sum(coords * coords, axis=1)[:, None] + target_sq[None, :] - inner
        return jax.nn.logsumexp(target_term[None, :] - cost / entropic_scale, axis=1)

    return (-entropic_scale * lax.map(one_block, blocks)).reshape(count)


def reference(sources, log_source_mass, targets, log_target_mass, start_potential):
    target_term = start_potential / entropic_scale + log_target_mass
    row_potential = jnp.zeros((sources.shape[1],), jnp.float32)
    column_potential = start_potential
    for sweep in range(ITERS):
        row_potential = row_sweep(sources, targets, target_term)
        source_term = row_potential / entropic_scale + log_source_mass
        column_potential = row_sweep(targets, sources, source_term)
        target_term = column_potential / entropic_scale + log_target_mass
    return row_potential, column_potential
```

```python
import functools
import math

import jax
import jax.numpy as jnp
from jax import lax
from jax.experimental import pallas as pl
from jax.experimental.pallas import tpu as pltpu
from jax.sharding import Mesh, PartitionSpec as P

LOG2E = math.log2(math.e)
LN2 = math.log(2.0)
LANES = 128
ROWS = 32
LEFT = (0, 0, 1, 1, 0, 2)
RIGHT = (0, 1, 0, 1, 2, 0)
LOWEST = -1e30
F32, BF16 = jnp.float32, jnp.bfloat16


def parts_of(value):
    first = value.astype(BF16)
    rest = value - first.astype(F32)
    second = rest.astype(BF16)
    third = (rest - second.astype(F32)).astype(BF16)
    return first, second, third


def merge(values):
    peak = jnp.max(values, axis=0)
    return peak + LOG2E * jnp.log(jnp.sum(jnp.exp2(values - peak[None]), axis=0))


def row_of(shape, row):
    return lax.broadcasted_iota(jnp.int32, shape, 0) == row


def with_row(block, row, value):
    return jnp.where(row_of(block.shape, row), value, block)


def fold(left_ref, right_ref, step):
    count, width = left_ref.shape[1], right_ref.shape[1]
    peak = jnp.full((8, width), LOWEST, F32)
    total = jnp.zeros((8, width), F32)
    for at in range(0, count, step):
        scores = lax.dot_general(
            left_ref[:, at : at + step],
            right_ref[...],
            (((0,), (0,)), ((), ())),
            preferred_element_type=F32,
        ).reshape(step // 8, 8, width)
        new_peak = jnp.maximum(peak, jnp.max(scores, axis=0))
        total = total * jnp.exp2(peak - new_peak) + jnp.sum(jnp.exp2(scores - new_peak[None]), axis=0)
        peak = new_peak
    top = jnp.max(peak, axis=0, keepdims=True)
    whole = jnp.sum(total * jnp.exp2(peak - top), axis=0, keepdims=True)
    return top + LOG2E * jnp.log(whole)


def as_rows(line):
    return [line[:, at : at + LANES] for at in range(0, line.shape[1], LANES)]


def send_to_all(line, out_ref):
    for at, piece in enumerate(as_rows(line)):
        out_ref[:, at, :] = jnp.broadcast_to(piece, (out_ref.shape[0], LANES))


def pack_kernel(src_ref, src_mass_ref, tgt_ref, tgt_mass_ref, start_ref, src_out, tgt_out):
    dims = src_ref.shape[0]
    block = jnp.concatenate([src_ref[...], src_mass_ref[...], jnp.zeros((1, LANES), F32)], axis=0)
    src_out[...] = jnp.broadcast_to(block[None], src_out.shape)
    tgt_out[...] = jnp.concatenate([tgt_ref[...], tgt_mass_ref[...], start_ref[...]], axis=0)


def set_beta(tgt_ref, at, beta):
    lanes = slice(at, at + beta.shape[1])
    for slot, part in enumerate(parts_of(beta)):
        rows = slice(slot * ROWS, slot * ROWS + ROWS)
        block = tgt_ref[rows, lanes].astype(F32)
        tgt_ref[rows, lanes] = with_row(block, ROWS - 2, part.astype(F32)).astype(BF16)


def first_kernel(dims, y_count, src_ref, *refs):
    tgt_refs = refs[:y_count]
    row_out, src_out, tgt_out, src_mass_out, tgt_mass_out = refs[y_count : y_count + 5]
    held = refs[y_count + 5]
    y = lax.axis_index("y")
    for shift in range(y_count):
        held[lax.rem(y + y_count - shift, y_count)] = tgt_refs[shift][...]
    groups = src_ref.shape[0]
    for group in range(groups):
        block = src_ref[group]
        src_mass_out[group : group + 1, :] = LOG2E * block[dims : dims + 1, :]
        spare = lax.broadcasted_iota(jnp.int32, block.shape, 0) >= dims
        split = parts_of(jnp.where(spare, 0.0, (0.5 * LOG2E) * block))
        lanes = slice(group * LANES, group * LANES + LANES)
        for slot, which in enumerate(LEFT):
            piece = split[which].astype(F32)
            if slot < 3:
                piece = with_row(piece, ROWS - 2, 1.0)
            src_out[slot * ROWS : slot * ROWS + ROWS, lanes] = piece.astype(BF16)
    width = held.shape[2]
    for group in range(y_count):
        block = held[group]
        mass = LOG2E * block[dims : dims + 1, :]
        for at, piece in enumerate(as_rows(mass)):
            row = group * (width // LANES) + at
            tgt_mass_out[row : row + 1, :] = piece
        spare = lax.broadcasted_iota(jnp.int32, block.shape, 0) >= dims
        coords = jnp.where(spare, 0.0, block)
        split = parts_of(coords)
        norm = jnp.sum(coords * coords, axis=0, keepdims=True)
        beta = mass + LOG2E * (0.5 * block[dims + 1 : dims + 2, :] - 0.25 * norm)
        beta_parts = parts_of(beta)
        lanes = slice(group * width, group * width + width)
        for slot, which in enumerate(RIGHT):
            piece = split[which].astype(F32)
            if slot < 3:
                piece = with_row(piece, ROWS - 2, beta_parts[slot].astype(F32))
                piece = with_row(piece, ROWS - 1, 1.0)
            tgt_out[slot * ROWS : slot * ROWS + ROWS, lanes] = piece.astype(BF16)
    send_to_all(fold(tgt_out, src_out, 512), row_out)


def column_line(rows_ref, src_ref, src_mass_ref, tgt_ref, own_src, step):
    merged = merge(rows_ref[...])
    alpha = src_mass_ref[...] - merged
    split = parts_of(alpha)
    own_src[...] = src_ref[...]
    for group in range(alpha.shape[0]):
        lanes = slice(group * LANES, group * LANES + LANES)
        for slot in range(3):
            rows = slice(slot * ROWS, slot * ROWS + ROWS)
            block = with_row(src_ref[rows, lanes].astype(F32), ROWS - 2, 0.0)
            value = split[slot][group : group + 1, :].astype(F32)
            own_src[rows, lanes] = with_row(block, ROWS - 1, value).astype(BF16)
    return merged, fold(own_src, tgt_ref, step)


def column_kernel(rows_ref, src_ref, src_mass_ref, tgt_ref, col_out, own_src):
    unused, line = column_line(rows_ref, src_ref, src_mass_ref, tgt_ref, own_src, 256)
    send_to_all(line, col_out)


def row_kernel(cols_ref, src_ref, tgt_ref, tgt_mass_ref, row_out, own_tgt):
    beta = tgt_mass_ref[...] - merge(cols_ref[...])
    own_tgt[...] = tgt_ref[...]
    for group in range(beta.shape[0]):
        set_beta(own_tgt, group * LANES, beta[group : group + 1, :])
    send_to_all(fold(own_tgt, src_ref, 512), row_out)


def last_column_kernel(
    x_axes, y_count, rows_ref, src_ref, src_mass_ref, tgt_ref, own_ref, col_out, pot_out, own_src, kept
):
    merged, line = column_line(rows_ref, src_ref, src_mass_ref, tgt_ref, own_src, 256)
    kept[...] = merged
    mine = kept[pl.ds(lax.axis_index(x_axes), 1), :]
    coords = own_ref[...]
    norm = jnp.sum(coords * coords, axis=0, keepdims=True)
    pot_out[...] = 0.5 * norm - (2.0 * LN2) * mine
    pieces = as_rows(line)
    share = len(pieces) // y_count
    for to in range(col_out.shape[0]):
        for at in range(share):
            col_out[to, at : at + 1, :] = pieces[(to % y_count) * share + at]


def final_kernel(cols_ref, tgt_ref, pot_out):
    merged = merge(cols_ref[...])
    coords = tgt_ref[...]
    norm = jnp.sum(coords * coords, axis=0, keepdims=True)
    for at, piece in enumerate(as_rows(norm)):
        pot_out[at : at + 1, :] = 0.5 * piece - (2.0 * LN2) * merged[at : at + 1, :]


def call(kernel, outs, scratch=()):
    return pl.pallas_call(
        kernel,
        out_shape=outs,
        scratch_shapes=list(scratch),
        compiler_params=pltpu.CompilerParams(vmem_limit_bytes=24 * 1024 * 1024),
    )


def shape(*dims, dtype=F32):
    return jax.ShapeDtypeStruct(dims, dtype)


def on_device(sources, log_source_mass, targets, log_target_mass, start_potential):
    near, far = ("x", "c"), ("z", "y")
    dims, own_rows = sources.shape
    own_cols = targets.shape[1]
    near_count, y_count = lax.axis_size(near), lax.axis_size("y")
    far_count = lax.axis_size(far)
    rows, cols = near_count * own_rows, y_count * own_cols
    row_tiles, col_tiles = rows // LANES, cols // LANES
    depth = len(LEFT) * ROWS

    def swap(value, axes):
        return lax.all_to_all(value, axes, 0, 0, tiled=True)

    src_send, tgt_own = call(pack_kernel, (shape(near_count, ROWS, LANES), shape(ROWS, own_cols)))(
        sources, log_source_mass[None], targets, log_target_mass[None], start_potential[None]
    )
    tgts = [tgt_own] + [
        lax.ppermute(tgt_own, "y", [(k, (k + shift) % y_count) for k in range(y_count)])
        for shift in range(1, y_count)
    ]
    src_all = swap(src_send, near)
    row_send, src, tgt, src_mass, tgt_mass = call(
        functools.partial(first_kernel, dims, y_count),
        (
            shape(near_count, row_tiles, LANES),
            shape(depth, rows, dtype=BF16),
            shape(depth, cols, dtype=BF16),
            shape(row_tiles, LANES),
            shape(col_tiles, LANES),
        ),
        [pltpu.VMEM((y_count, ROWS, own_cols), F32)],
    )(src_all, *tgts)
    row_all = swap(row_send, near)
    col_send = call(
        column_kernel, shape(far_count, col_tiles, LANES), [pltpu.VMEM((depth, rows), BF16)]
    )(row_all, src, src_mass, tgt)
    col_all = swap(col_send, far)
    row_send = call(
        row_kernel, shape(near_count, row_tiles, LANES), [pltpu.VMEM((depth, cols), BF16)]
    )(col_all, src, tgt, tgt_mass)
    row_all = swap(row_send, near)
    col_send, row_potential = call(
        functools.partial(last_column_kernel, near, y_count),
        (shape(far_count, own_cols // LANES, LANES), shape(1, own_rows)),
        [pltpu.VMEM((depth, rows), BF16), pltpu.VMEM((row_tiles, LANES), F32)],
    )(row_all, src, src_mass, tgt, sources)
    col_all = swap(col_send, far)
    column_potential = call(final_kernel, shape(own_cols // LANES, LANES))(col_all, targets)
    return row_potential.reshape(own_rows), column_potential.reshape(own_cols)


def solution(mesh):
    split = Mesh(mesh.devices.reshape(8, 4, 4, 2), ("z", "y", "x", "c"))
    everywhere, column = ("z", "y", "x", "c"), ("y", "x", "c")
    return jax.shard_map(
        on_device,
        mesh=split,
        in_specs=(P(None, everywhere), P(everywhere), P(None, column), P(column), P(column)),
        out_specs=(P(everywhere), P(column)),
        check_vma=False,
    )
```

```python
import functools
import math

import jax
import jax.numpy as jnp
from jax import lax
from jax.experimental import pallas as pl
from jax.experimental.pallas import tpu as pltpu
from jax.sharding import Mesh, PartitionSpec as P


LOG2E = math.log2(math.e)
LN2 = math.log(2.0)
LANES = 128
ROWS = 32
LEFT = (0, 0, 1, 1, 0, 2)
RIGHT = (0, 1, 0, 1, 2, 0)
LOWEST = -1e30
F32, BF16 = jnp.float32, jnp.bfloat16


def parts_of(value):
    first = value.astype(BF16)
    rest = value - first.astype(F32)
    second = rest.astype(BF16)
    third = (rest - second.astype(F32)).astype(BF16)
    return first, second, third


def merge(values):
    peak = jnp.max(values, axis=0)
    return peak + LOG2E * jnp.log(jnp.sum(jnp.exp2(values - peak[None]), axis=0))


def row_of(shape, row):
    return lax.broadcasted_iota(jnp.int32, shape, 0) == row


def with_row(block, row, value):
    return jnp.where(row_of(block.shape, row), value, block)


def fold(left_ref, right_ref, step):
    count, width = left_ref.shape[1], right_ref.shape[1]
    peak = jnp.full((8, width), LOWEST, F32)
    total = jnp.zeros((8, width), F32)
    for at in range(0, count, step):
        scores = lax.dot_general(
            left_ref[:, at : at + step],
            right_ref[...],
            (((0,), (0,)), ((), ())),
            preferred_element_type=F32,
        ).reshape(step // 8, 8, width)
        new_peak = jnp.maximum(peak, jnp.max(scores, axis=0))
        total = total * jnp.exp2(peak - new_peak) + jnp.sum(jnp.exp2(scores - new_peak[None]), axis=0)
        peak = new_peak
    top = jnp.max(peak, axis=0, keepdims=True)
    whole = jnp.sum(total * jnp.exp2(peak - top), axis=0, keepdims=True)
    return top + LOG2E * jnp.log(whole)


def as_rows(line):
    return [line[:, at : at + LANES] for at in range(0, line.shape[1], LANES)]


def send_to_all(line, out_ref):
    for at, piece in enumerate(as_rows(line)):
        out_ref[:, at, :] = jnp.broadcast_to(piece, (out_ref.shape[0], LANES))


def pack_kernel(*refs):
    inputs, (src_out, tgt_out), held, sems = refs[:5], refs[5:7], refs[7:12], refs[12]
    copies = [
        pltpu.make_async_copy(whence, where, sems.at[at])
        for at, (whence, where) in enumerate(zip(inputs, held))
    ]
    for copy in copies:
        copy.start()
    for copy in copies:
        copy.wait()
    src, src_mass, tgt, tgt_mass, start = (ref[...] for ref in held)
    tgt_out[...] = jnp.concatenate([tgt, tgt_mass, start], axis=0)
    block = jnp.concatenate([src, src_mass, jnp.zeros((1, LANES), F32)], axis=0)
    src_out[...] = jnp.broadcast_to(block[None], src_out.shape)


def set_beta(tgt_ref, at, beta):
    lanes = slice(at, at + beta.shape[1])
    for slot, part in enumerate(parts_of(beta)):
        rows = slice(slot * ROWS, slot * ROWS + ROWS)
        block = tgt_ref[rows, lanes].astype(F32)
        tgt_ref[rows, lanes] = with_row(block, ROWS - 2, part.astype(F32)).astype(BF16)


def first_kernel(dims, share_count, src_ref, *refs):
    tgt_refs = refs[:share_count]
    row_out, src_out, tgt_out, src_mass_out, tgt_mass_out = refs[share_count : share_count + 5]
    held = refs[share_count + 5]
    mine = lax.axis_index("c")
    for shift in range(share_count):
        held[lax.rem(mine + share_count - shift, share_count)] = tgt_refs[shift][...]
    groups = src_ref.shape[0]
    for group in range(groups):
        block = src_ref[group]
        src_mass_out[group : group + 1, :] = LOG2E * block[dims : dims + 1, :]
        spare = lax.broadcasted_iota(jnp.int32, block.shape, 0) >= dims
        split = parts_of(jnp.where(spare, 0.0, (0.5 * LOG2E) * block))
        lanes = slice(group * LANES, group * LANES + LANES)
        for slot, which in enumerate(LEFT):
            piece = split[which].astype(F32)
            if slot < 3:
                piece = with_row(piece, ROWS - 2, 1.0)
            src_out[slot * ROWS : slot * ROWS + ROWS, lanes] = piece.astype(BF16)
    width = held.shape[2]
    for group in range(share_count):
        block = held[group]
        mass = LOG2E * block[dims : dims + 1, :]
        for at, piece in enumerate(as_rows(mass)):
            row = group * (width // LANES) + at
            tgt_mass_out[row : row + 1, :] = piece
        spare = lax.broadcasted_iota(jnp.int32, block.shape, 0) >= dims
        coords = jnp.where(spare, 0.0, block)
        split = parts_of(coords)
        norm = jnp.sum(coords * coords, axis=0, keepdims=True)
        beta = mass + LOG2E * (0.5 * block[dims + 1 : dims + 2, :] - 0.25 * norm)
        beta_parts = parts_of(beta)
        lanes = slice(group * width, group * width + width)
        for slot, which in enumerate(RIGHT):
            piece = split[which].astype(F32)
            if slot < 3:
                piece = with_row(piece, ROWS - 2, beta_parts[slot].astype(F32))
                piece = with_row(piece, ROWS - 1, 1.0)
            tgt_out[slot * ROWS : slot * ROWS + ROWS, lanes] = piece.astype(BF16)
    send_to_all(fold(tgt_out, src_out, 256), row_out)


def column_line(rows_ref, src_ref, src_mass_ref, tgt_ref, own_src, step):
    merged = merge(rows_ref[...])
    alpha = src_mass_ref[...] - merged
    split = parts_of(alpha)
    own_src[...] = src_ref[...]
    for group in range(alpha.shape[0]):
        lanes = slice(group * LANES, group * LANES + LANES)
        for slot in range(3):
            rows = slice(slot * ROWS, slot * ROWS + ROWS)
            block = with_row(src_ref[rows, lanes].astype(F32), ROWS - 2, 0.0)
            value = split[slot][group : group + 1, :].astype(F32)
            own_src[rows, lanes] = with_row(block, ROWS - 1, value).astype(BF16)
    return merged, fold(own_src, tgt_ref, step)


def column_kernel(rows_ref, src_ref, src_mass_ref, tgt_ref, col_out, own_src):
    _, line = column_line(rows_ref, src_ref, src_mass_ref, tgt_ref, own_src, 512)
    send_to_all(line, col_out)


def row_kernel(cols_ref, src_ref, tgt_ref, tgt_mass_ref, row_out, own_tgt):
    beta = tgt_mass_ref[...] - merge(cols_ref[...])
    own_tgt[...] = tgt_ref[...]
    for group in range(beta.shape[0]):
        set_beta(own_tgt, group * LANES, beta[group : group + 1, :])
    send_to_all(fold(own_tgt, src_ref, 256), row_out)


def last_column_kernel(
    near, share_count, rows_ref, src_ref, src_mass_ref, tgt_ref, own_ref, col_out, pot_out, own_src, kept
):
    merged, line = column_line(rows_ref, src_ref, src_mass_ref, tgt_ref, own_src, 512)
    kept[...] = merged
    mine = kept[pl.ds(lax.axis_index(near), 1), :]
    coords = own_ref[...]
    norm = jnp.sum(coords * coords, axis=0, keepdims=True)
    pot_out[...] = 0.5 * norm - (2.0 * LN2) * mine
    pieces = as_rows(line)
    share = len(pieces) // share_count
    for to in range(col_out.shape[0]):
        for at in range(share):
            col_out[to, at : at + 1, :] = pieces[(to % share_count) * share + at]


def final_kernel(cols_ref, tgt_ref, pot_out):
    merged = merge(cols_ref[...])
    coords = tgt_ref[...]
    norm = jnp.sum(coords * coords, axis=0, keepdims=True)
    for at, piece in enumerate(as_rows(norm)):
        pot_out[at : at + 1, :] = 0.5 * piece - (2.0 * LN2) * merged[at : at + 1, :]


def call(kernel, outs, scratch=(), mib=24, **more):
    return pl.pallas_call(
        kernel,
        out_shape=outs,
        **more,
        scratch_shapes=list(scratch),
        compiler_params=pltpu.CompilerParams(vmem_limit_bytes=mib * 1024 * 1024),
    )


def shape(*dims, dtype=F32):
    return jax.ShapeDtypeStruct(dims, dtype)


def on_device(sources, log_source_mass, targets, log_target_mass, start_potential):
    near, far = ("y", "x"), ("z", "c")
    dims, own_rows = sources.shape
    own_cols = targets.shape[1]
    near_count, share_count = lax.axis_size(near), lax.axis_size("c")
    far_count = lax.axis_size(far)
    rows, cols = near_count * own_rows, share_count * own_cols
    row_tiles, col_tiles = rows // LANES, cols // LANES
    depth = len(LEFT) * ROWS

    def swap(value, axes):
        return lax.all_to_all(value, axes, 0, 0, tiled=True)

    given = (sources, log_source_mass[None], targets, log_target_mass[None], start_potential[None])
    src_send, tgt_own = call(
        pack_kernel,
        (shape(near_count, ROWS, LANES), shape(ROWS, own_cols)),
        [pltpu.VMEM(array.shape, F32) for array in given] + [pltpu.SemaphoreType.DMA((len(given),))],
        mib=60,
        in_specs=[pl.BlockSpec(memory_space=pl.ANY)] * len(given),
    )(*given)
    tgts = [tgt_own] + [
        lax.ppermute(tgt_own, "c", [(k, (k + shift) % share_count) for k in range(share_count)])
        for shift in range(1, share_count)
    ]
    src_all = swap(src_send, near)
    row_send, src, tgt, src_mass, tgt_mass = call(
        functools.partial(first_kernel, dims, share_count),
        (
            shape(near_count, row_tiles, LANES),
            shape(depth, rows, dtype=BF16),
            shape(depth, cols, dtype=BF16),
            shape(row_tiles, LANES),
            shape(col_tiles, LANES),
        ),
        [pltpu.VMEM((share_count, ROWS, own_cols), F32)],
    )(src_all, *tgts)
    row_all = swap(row_send, near)
    col_send = call(
        column_kernel, shape(far_count, col_tiles, LANES), [pltpu.VMEM((depth, rows), BF16)]
    )(row_all, src, src_mass, tgt)
    col_all = swap(col_send, far)
    row_send = call(
        row_kernel, shape(near_count, row_tiles, LANES), [pltpu.VMEM((depth, cols), BF16)]
    )(col_all, src, tgt, tgt_mass)
    row_all = swap(row_send, near)
    col_send, row_potential = call(
        functools.partial(last_column_kernel, near, share_count),
        (shape(far_count, own_cols // LANES, LANES), shape(1, own_rows)),
        [pltpu.VMEM((depth, rows), BF16), pltpu.VMEM((row_tiles, LANES), F32)],
    )(row_all, src, src_mass, tgt, sources)
    col_all = swap(col_send, far)
    column_potential = call(final_kernel, shape(own_cols // LANES, LANES))(col_all, targets)
    return row_potential.reshape(own_rows), column_potential.reshape(own_cols)


def solution(mesh):
    split = Mesh(mesh.devices.reshape(8, 4, 4, 2), ("z", "y", "x", "c"))
    everywhere, column = ("z", "y", "x", "c"), ("y", "x", "c")
    return jax.shard_map(
        on_device,
        mesh=split,
        in_specs=(P(None, everywhere), P(everywhere), P(None, column), P(column), P(column)),
        out_specs=(P(everywhere), P(column)),
        check_vma=False,
    )
```

```python
import functools
import math

import jax
import jax.numpy as jnp
from jax import lax
from jax.experimental import pallas as pl
from jax.experimental.pallas import tpu as pltpu
from jax.sharding import Mesh, PartitionSpec as P


LOG2E = math.log2(math.e)
LN2 = math.log(2.0)
LANES = 128
TILE = 256
STEP = 128
ROWS = 32
LEFT = (0, 0, 1, 1, 0, 2)
RIGHT = (0, 1, 0, 1, 2, 0)
F32, BF16 = jnp.float32, jnp.bfloat16


def parts_of(value):
    first = value.astype(BF16)
    rest = value - first.astype(F32)
    second = rest.astype(BF16)
    third = (rest - second.astype(F32)).astype(BF16)
    return first, second, third


def merge(values):
    peak = jnp.max(values, axis=0)
    return peak + LOG2E * jnp.log(jnp.sum(jnp.exp2(values - peak[None]), axis=0))


def row_of(shape, row):
    return lax.broadcasted_iota(jnp.int32, shape, 0) == row


def with_row(block, row, value):
    return jnp.where(row_of(block.shape, row), value, block)


def fold(left, count, right_ref, step=STEP, tile=TILE):
    items = [(lane, at) for lane in range(0, right_ref.shape[1], tile) for at in range(0, count, step)]

    def scores_of(lane, at):
        return lax.dot_general(
            left(slice(at, at + step)),
            right_ref[:, lane : lane + tile],
            (((0,), (0,)), ((), ())),
            preferred_element_type=F32,
        ).reshape(step // 8, 8, tile)

    lines = []
    coming = scores_of(*items[0])
    for number, (lane, at) in enumerate(items):
        scores = coming
        if number + 1 < len(items):
            coming = scores_of(*items[number + 1])
        if at == 0:
            peak = jnp.max(scores, axis=0)
            total = jnp.sum(jnp.exp2(scores - peak[None]), axis=0)
        else:
            new_peak = jnp.maximum(peak, jnp.max(scores, axis=0))
            total = total * jnp.exp2(peak - new_peak) + jnp.sum(jnp.exp2(scores - new_peak[None]), axis=0)
            peak = new_peak
        if at + step == count:
            top = jnp.max(peak, axis=0, keepdims=True)
            whole = jnp.sum(total * jnp.exp2(peak - top), axis=0, keepdims=True)
            lines.append(top + LOG2E * jnp.log(whole))
    return jnp.concatenate(lines, axis=1)


def patched(own_ref, ref):
    return lambda lanes: jnp.concatenate([own_ref[:, lanes], ref[own_ref.shape[0] :, lanes]], axis=0)


def as_rows(line):
    return [line[:, at : at + LANES] for at in range(0, line.shape[1], LANES)]


def send_to_all(line, out_ref):
    for at, piece in enumerate(as_rows(line)):
        out_ref[:, at, :] = jnp.broadcast_to(piece, (out_ref.shape[0], LANES))


def pack_kernel(*refs):
    inputs, (src_out, tgt_out), held, sems = refs[:5], refs[5:7], refs[7:12], refs[12]
    copies = [
        pltpu.make_async_copy(whence, where, sems.at[at])
        for at, (whence, where) in enumerate(zip(inputs, held))
    ]
    for copy in copies:
        copy.start()
    for copy in copies:
        copy.wait()
    src, src_mass, tgt, tgt_mass, start = (ref[...] for ref in held)
    tgt_out[...] = jnp.concatenate([tgt, tgt_mass, start], axis=0)
    block = jnp.concatenate([src, src_mass, jnp.zeros((1, LANES), F32)], axis=0)
    src_out[...] = jnp.broadcast_to(block[None], src_out.shape)


def first_kernel(dims, share_count, src_ref, *refs):
    tgt_refs = refs[:share_count]
    row_out, src_out, tgt_out, src_mass_out, tgt_mass_out = refs[share_count : share_count + 5]
    held = refs[share_count + 5]
    mine = lax.axis_index("c")
    for shift in range(share_count):
        held[lax.rem(mine + share_count - shift, share_count)] = tgt_refs[shift][...]
    groups = src_ref.shape[0]
    for group in range(groups):
        block = src_ref[group]
        src_mass_out[group : group + 1, :] = LOG2E * block[dims : dims + 1, :]
        spare = lax.broadcasted_iota(jnp.int32, block.shape, 0) >= dims
        split = parts_of(jnp.where(spare, 0.0, (0.5 * LOG2E) * block))
        lanes = slice(group * LANES, group * LANES + LANES)
        for slot, which in enumerate(LEFT):
            piece = split[which].astype(F32)
            if slot < 3:
                piece = with_row(piece, ROWS - 2, 1.0)
            src_out[slot * ROWS : slot * ROWS + ROWS, lanes] = piece.astype(BF16)
    width = held.shape[2]
    for group in range(share_count):
        block = held[group]
        mass = LOG2E * block[dims : dims + 1, :]
        for at, piece in enumerate(as_rows(mass)):
            row = group * (width // LANES) + at
            tgt_mass_out[row : row + 1, :] = piece
        spare = lax.broadcasted_iota(jnp.int32, block.shape, 0) >= dims
        coords = jnp.where(spare, 0.0, block)
        split = parts_of(coords)
        norm = jnp.sum(coords * coords, axis=0, keepdims=True)
        beta = mass + LOG2E * (0.5 * block[dims + 1 : dims + 2, :] - 0.25 * norm)
        beta_parts = parts_of(beta)
        lanes = slice(group * width, group * width + width)
        for slot, which in enumerate(RIGHT):
            piece = split[which].astype(F32)
            if slot < 3:
                piece = with_row(piece, ROWS - 2, beta_parts[slot].astype(F32))
                piece = with_row(piece, ROWS - 1, 1.0)
            tgt_out[slot * ROWS : slot * ROWS + ROWS, lanes] = piece.astype(BF16)
    send_to_all(fold(lambda lanes: tgt_out[:, lanes], tgt_out.shape[1], src_out), row_out)


def set_terms(own_ref, ref, values, cleared, row):
    split = parts_of(values)
    for group in range(values.shape[0]):
        lanes = slice(group * LANES, group * LANES + LANES)
        for slot in range(3):
            rows = slice(slot * ROWS, slot * ROWS + ROWS)
            block = ref[rows, lanes].astype(F32)
            if cleared is not None:
                block = with_row(block, cleared, 0.0)
            own_ref[rows, lanes] = with_row(block, row, split[slot][group : group + 1, :].astype(F32)).astype(BF16)


def column_line(merged, src_ref, src_mass_ref, tgt_ref, own_src):
    set_terms(own_src, src_ref, src_mass_ref[...] - merged, ROWS - 2, ROWS - 1)
    return fold(patched(own_src, src_ref), src_ref.shape[1], tgt_ref)


def column_kernel(rows_ref, src_ref, src_mass_ref, tgt_ref, col_out, own_src):
    send_to_all(column_line(merge(rows_ref[...]), src_ref, src_mass_ref, tgt_ref, own_src), col_out)


def row_kernel(cols_ref, src_ref, tgt_ref, tgt_mass_ref, row_out, own_tgt):
    set_terms(own_tgt, tgt_ref, tgt_mass_ref[...] - merge(cols_ref[...]), None, ROWS - 2)
    send_to_all(fold(patched(own_tgt, tgt_ref), tgt_ref.shape[1], src_ref), row_out)


def last_column_kernel(share_count, rows_ref, src_ref, src_mass_ref, tgt_ref, col_out, merged_out, own_src):
    merged = merge(rows_ref[...])
    merged_out[...] = merged
    pieces = as_rows(column_line(merged, src_ref, src_mass_ref, tgt_ref, own_src))
    share = len(pieces) // share_count
    for part in range(share_count):
        block = jnp.concatenate(pieces[part * share : part * share + share], axis=0)
        for to in range(part, col_out.shape[0], share_count):
            col_out[to] = block


def final_kernel(near, cols_ref, rows_ref, src_ref, tgt_ref, row_out, pot_out):
    mine = rows_ref[pl.ds(lax.axis_index(near), 1), :]
    coords = src_ref[...]
    norm = jnp.sum(coords * coords, axis=0, keepdims=True)
    row_out[...] = 0.5 * norm - (2.0 * LN2) * mine
    merged = merge(cols_ref[...])
    coords = tgt_ref[...]
    norm = jnp.sum(coords * coords, axis=0, keepdims=True)
    for at, piece in enumerate(as_rows(norm)):
        pot_out[at : at + 1, :] = 0.5 * piece - (2.0 * LN2) * merged[at : at + 1, :]


def call(kernel, outs, scratch=(), mib=24, **more):
    return pl.pallas_call(
        kernel,
        out_shape=outs,
        **more,
        scratch_shapes=list(scratch),
        compiler_params=pltpu.CompilerParams(vmem_limit_bytes=mib * 1024 * 1024),
    )


def shape(*dims, dtype=F32):
    return jax.ShapeDtypeStruct(dims, dtype)


def on_device(sources, log_source_mass, targets, log_target_mass, start_potential):
    near, far = ("y", "x"), ("z", "c")
    dims, own_rows = sources.shape
    own_cols = targets.shape[1]
    near_count, share_count = lax.axis_size(near), lax.axis_size("c")
    far_count = lax.axis_size(far)
    rows, cols = near_count * own_rows, share_count * own_cols
    row_tiles, col_tiles = rows // LANES, cols // LANES
    depth = len(LEFT) * ROWS

    def swap(value, axes):
        return lax.all_to_all(value, axes, 0, 0, tiled=True)

    given = (sources, log_source_mass[None], targets, log_target_mass[None], start_potential[None])
    src_send, tgt_own = call(
        pack_kernel,
        (shape(near_count, ROWS, LANES), shape(ROWS, own_cols)),
        [pltpu.VMEM(array.shape, F32) for array in given] + [pltpu.SemaphoreType.DMA((len(given),))],
        in_specs=[pl.BlockSpec(memory_space=pl.ANY)] * len(given),
    )(*[pltpu.with_memory_space_constraint(array, pltpu.HBM) for array in given])
    tgts = [tgt_own] + [
        lax.ppermute(tgt_own, "c", [(k, (k + shift) % share_count) for k in range(share_count)])
        for shift in range(1, share_count)
    ]
    src_all = swap(src_send, near)
    row_send, src, tgt, src_mass, tgt_mass = call(
        functools.partial(first_kernel, dims, share_count),
        (
            shape(near_count, row_tiles, LANES),
            shape(depth, rows, dtype=BF16),
            shape(depth, cols, dtype=BF16),
            shape(row_tiles, LANES),
            shape(col_tiles, LANES),
        ),
        [pltpu.VMEM((share_count, ROWS, own_cols), F32)],
    )(src_all, *tgts)
    changed = 3 * ROWS
    row_all = swap(row_send, near)
    col_send = call(
        column_kernel, shape(far_count, col_tiles, LANES), [pltpu.VMEM((changed, rows), BF16)]
    )(row_all, src, src_mass, tgt)
    col_all = swap(col_send, far)
    row_send = call(
        row_kernel, shape(near_count, row_tiles, LANES), [pltpu.VMEM((changed, cols), BF16)]
    )(col_all, src, tgt, tgt_mass)
    row_all = swap(row_send, near)
    col_send, merged = call(
        functools.partial(last_column_kernel, share_count),
        (shape(far_count, own_cols // LANES, LANES), shape(row_tiles, LANES)),
        [pltpu.VMEM((changed, rows), BF16)],
    )(row_all, src, src_mass, tgt)
    col_all = swap(col_send, far)
    row_potential, column_potential = call(
        functools.partial(final_kernel, near), (shape(1, own_rows), shape(own_cols // LANES, LANES))
    )(col_all, merged, sources, targets)
    return row_potential.reshape(own_rows), column_potential.reshape(own_cols)


def solution(mesh):
    split = Mesh(mesh.devices.reshape(8, 4, 4, 2), ("z", "y", "x", "c"))
    everywhere, column = ("z", "y", "x", "c"), ("y", "x", "c")
    return jax.shard_map(
        on_device,
        mesh=split,
        in_specs=(P(None, everywhere), P(everywhere), P(None, column), P(column), P(column)),
        out_specs=(P(everywhere), P(column)),
        check_vma=False,
    )
```

```python
import functools
import math

import jax
import jax.numpy as jnp
from jax import lax
from jax.experimental import pallas as pl
from jax.experimental.pallas import tpu as pltpu
from jax.sharding import Mesh, PartitionSpec as P


LOG2E = math.log2(math.e)
LN2 = math.log(2.0)
LANES = 128
TILE = 256
STEP = 128
PLAN_STEP = 512
SMALLEST = 2.0**-90
ROWS = 32
LEFT = (0, 0, 1, 1, 0, 2)
RIGHT = (0, 1, 0, 1, 2, 0)
F32, BF16 = jnp.float32, jnp.bfloat16


def parts_of(value):
    first = value.astype(BF16)
    rest = value - first.astype(F32)
    second = rest.astype(BF16)
    third = (rest - second.astype(F32)).astype(BF16)
    return first, second, third


def merge(values):
    peak = jnp.max(values, axis=0)
    return peak + LOG2E * jnp.log(jnp.sum(jnp.exp2(values - peak[None]), axis=0))


def row_of(shape, row):
    return lax.broadcasted_iota(jnp.int32, shape, 0) == row


def with_row(block, row, value):
    return jnp.where(row_of(block.shape, row), value, block)


def fold(left, count, right, width, step=STEP, tile=TILE):
    items = [(lane, at) for lane in range(0, width, tile) for at in range(0, count, step)]

    def scores_of(lane, at):
        return lax.dot_general(
            left(slice(at, at + step)),
            right(slice(lane, lane + tile)),
            (((0,), (0,)), ((), ())),
            preferred_element_type=F32,
        ).reshape(step // 8, 8, tile)

    lines = []
    coming = scores_of(*items[0])
    for number, (lane, at) in enumerate(items):
        scores = coming
        if number + 1 < len(items):
            coming = scores_of(*items[number + 1])
        if at == 0:
            peak = jnp.max(scores, axis=0)
            total = jnp.sum(jnp.exp2(scores - peak[None]), axis=0)
        else:
            new_peak = jnp.maximum(peak, jnp.max(scores, axis=0))
            total = total * jnp.exp2(peak - new_peak) + jnp.sum(jnp.exp2(scores - new_peak[None]), axis=0)
            peak = new_peak
        if at + step == count:
            top = jnp.max(peak, axis=0, keepdims=True)
            whole = jnp.sum(total * jnp.exp2(peak - top), axis=0, keepdims=True)
            lines.append(top + LOG2E * jnp.log(whole))
    return jnp.concatenate(lines, axis=1)


def plan_line(left, count, right, width, line_ref):
    lines = []
    for lane in range(0, width, TILE):
        total = jnp.zeros((8, TILE), F32)
        for at in range(0, count, PLAN_STEP):
            scores = lax.dot_general(
                left(slice(at, at + PLAN_STEP)),
                right(slice(lane, lane + TILE)),
                (((0,), (0,)), ((), ())),
                preferred_element_type=F32,
            ).reshape(PLAN_STEP // 8, 8, TILE)
            total = total + jnp.sum(jnp.exp2(scores), axis=0)
        lines.append(jnp.sum(total, axis=0, keepdims=True))
    set_rows(line_ref, jnp.concatenate(lines, axis=1), 0)
    sums = line_ref[...]
    line_ref[...] = LOG2E * jnp.log(sums)

    @pl.when(jnp.min(sums) < SMALLEST)
    def again():
        set_rows(line_ref, fold(left, count, right, width), 0)


def whole(ref):
    return lambda lanes: ref[:, lanes]


def patched(own_ref, ref):
    return lambda lanes: jnp.concatenate([own_ref[:, lanes], ref[own_ref.shape[0] :, lanes]], axis=0)


def as_rows(line):
    return [line[:, at : at + LANES] for at in range(0, line.shape[1], LANES)]


def set_rows(ref, line, row):
    for at, piece in enumerate(as_rows(line)):
        ref[row + at : row + at + 1, :] = piece


def send_to_all(line, out_ref):
    for at, piece in enumerate(as_rows(line)):
        out_ref[:, at, :] = jnp.broadcast_to(piece, (out_ref.shape[0], LANES))


def pack_kernel(*refs):
    inputs, (src_out, tgt_out), held, sems = refs[:5], refs[5:7], refs[7:12], refs[12]
    copies = [
        pltpu.make_async_copy(whence, where, sems.at[at])
        for at, (whence, where) in enumerate(zip(inputs, held))
    ]
    for copy in copies:
        copy.start()
    for copy in copies:
        copy.wait()
    src, src_mass, tgt, tgt_mass, start = (ref[...] for ref in held)
    tgt_out[...] = jnp.concatenate([tgt, tgt_mass, start], axis=0)
    block = jnp.concatenate([src, src_mass, jnp.zeros((1, LANES), F32)], axis=0)
    src_out[...] = jnp.broadcast_to(block[None], src_out.shape)


def first_kernel(dims, share_count, src_ref, *refs):
    tgt_refs = refs[:share_count]
    row_out, src_out, tgt_out, src_mass_out, tgt_mass_out, beta_out = refs[share_count : share_count + 6]
    held = refs[share_count + 6]
    mine = lax.axis_index("c")
    for shift in range(share_count):
        held[lax.rem(mine + share_count - shift, share_count)] = tgt_refs[shift][...]
    groups = src_ref.shape[0]
    for group in range(groups):
        block = src_ref[group]
        src_mass_out[group : group + 1, :] = LOG2E * block[dims : dims + 1, :]
        spare = lax.broadcasted_iota(jnp.int32, block.shape, 0) >= dims
        split = parts_of(jnp.where(spare, 0.0, (0.5 * LOG2E) * block))
        lanes = slice(group * LANES, group * LANES + LANES)
        for slot, which in enumerate(LEFT):
            piece = split[which].astype(F32)
            if slot < 3:
                piece = with_row(piece, ROWS - 2, 1.0)
            src_out[slot * ROWS : slot * ROWS + ROWS, lanes] = piece.astype(BF16)
    width = held.shape[2]
    for group in range(share_count):
        block = held[group]
        mass = LOG2E * block[dims : dims + 1, :]
        set_rows(tgt_mass_out, mass, group * (width // LANES))
        spare = lax.broadcasted_iota(jnp.int32, block.shape, 0) >= dims
        coords = jnp.where(spare, 0.0, block)
        split = parts_of(coords)
        norm = jnp.sum(coords * coords, axis=0, keepdims=True)
        beta = mass + LOG2E * (0.5 * block[dims + 1 : dims + 2, :] - 0.25 * norm)
        set_rows(beta_out, beta, group * (width // LANES))
        beta_parts = parts_of(beta)
        lanes = slice(group * width, group * width + width)
        for slot, which in enumerate(RIGHT):
            piece = split[which].astype(F32)
            if slot < 3:
                piece = with_row(piece, ROWS - 2, beta_parts[slot].astype(F32))
                piece = with_row(piece, ROWS - 1, 1.0)
            tgt_out[slot * ROWS : slot * ROWS + ROWS, lanes] = piece.astype(BF16)
    send_to_all(fold(whole(tgt_out), tgt_out.shape[1], whole(src_out), src_out.shape[1]), row_out)


def set_terms(own_ref, ref, values, row):
    split = parts_of(values)
    for group in range(values.shape[0]):
        lanes = slice(group * LANES, group * LANES + LANES)
        for slot in range(3):
            rows = slice(slot * ROWS, slot * ROWS + ROWS)
            block = ref[rows, lanes].astype(F32)
            own_ref[rows, lanes] = with_row(block, row, split[slot][group : group + 1, :].astype(F32)).astype(BF16)


def column_kernel(rows_ref, src_ref, src_mass_ref, tgt_ref, beta_ref, col_out, alpha_out, own_src, line_ref):
    alpha = src_mass_ref[...] - merge(rows_ref[...])
    alpha_out[...] = alpha
    set_terms(own_src, src_ref, alpha, ROWS - 1)
    plan_line(patched(own_src, src_ref), src_ref.shape[1], whole(tgt_ref), tgt_ref.shape[1], line_ref)
    col_out[...] = jnp.broadcast_to((line_ref[...] - beta_ref[...])[None], col_out.shape)


def row_kernel(
    cols_ref, own_src, src_ref, tgt_ref, tgt_mass_ref, alpha_ref, row_out, own_tgt, beta_out, line_ref
):
    beta = tgt_mass_ref[...] - merge(cols_ref[...])
    beta_out[...] = beta
    set_terms(own_tgt, tgt_ref, beta, ROWS - 2)
    plan_line(
        patched(own_tgt, tgt_ref), tgt_ref.shape[1], patched(own_src, src_ref), src_ref.shape[1], line_ref
    )
    row_out[...] = jnp.broadcast_to((line_ref[...] - alpha_ref[...])[None], row_out.shape)


def last_column_kernel(
    share_count, rows_ref, src_ref, src_mass_ref, own_tgt, tgt_ref, beta_ref, col_out, merged_out, own_src, line_ref
):
    merged = merge(rows_ref[...])
    merged_out[...] = merged
    set_terms(own_src, src_ref, src_mass_ref[...] - merged, ROWS - 1)
    plan_line(
        patched(own_src, src_ref), src_ref.shape[1], patched(own_tgt, tgt_ref), tgt_ref.shape[1], line_ref
    )
    line = line_ref[...] - beta_ref[...]
    share = line.shape[0] // share_count
    for part in range(share_count):
        for to in range(part, col_out.shape[0], share_count):
            col_out[to] = line[part * share : part * share + share]


def final_kernel(near, cols_ref, rows_ref, src_ref, tgt_ref, row_out, pot_out):
    mine = rows_ref[pl.ds(lax.axis_index(near), 1), :]
    coords = src_ref[...]
    norm = jnp.sum(coords * coords, axis=0, keepdims=True)
    row_out[...] = 0.5 * norm - (2.0 * LN2) * mine
    merged = merge(cols_ref[...])
    coords = tgt_ref[...]
    norm = jnp.sum(coords * coords, axis=0, keepdims=True)
    for at, piece in enumerate(as_rows(norm)):
        pot_out[at : at + 1, :] = 0.5 * piece - (2.0 * LN2) * merged[at : at + 1, :]


def call(kernel, outs, scratch=(), mib=24, **more):
    return pl.pallas_call(
        kernel,
        out_shape=outs,
        **more,
        scratch_shapes=list(scratch),
        compiler_params=pltpu.CompilerParams(vmem_limit_bytes=mib * 1024 * 1024),
    )


def shape(*dims, dtype=F32):
    return jax.ShapeDtypeStruct(dims, dtype)


def on_device(sources, log_source_mass, targets, log_target_mass, start_potential):
    near, far = ("y", "x"), ("z", "c")
    dims, own_rows = sources.shape
    own_cols = targets.shape[1]
    near_count, share_count = lax.axis_size(near), lax.axis_size("c")
    far_count = lax.axis_size(far)
    rows, cols = near_count * own_rows, share_count * own_cols
    row_tiles, col_tiles = rows // LANES, cols // LANES
    depth = len(LEFT) * ROWS

    def swap(value, axes):
        return lax.all_to_all(value, axes, 0, 0, tiled=True)

    given = (sources, log_source_mass[None], targets, log_target_mass[None], start_potential[None])
    src_send, tgt_own = call(
        pack_kernel,
        (shape(near_count, ROWS, LANES), shape(ROWS, own_cols)),
        [pltpu.VMEM(array.shape, F32) for array in given] + [pltpu.SemaphoreType.DMA((len(given),))],
        in_specs=[pl.BlockSpec(memory_space=pl.ANY)] * len(given),
    )(*[pltpu.with_memory_space_constraint(array, pltpu.HBM) for array in given])
    tgts = [tgt_own] + [
        lax.ppermute(tgt_own, "c", [(k, (k + shift) % share_count) for k in range(share_count)])
        for shift in range(1, share_count)
    ]
    src_all = swap(src_send, near)
    row_send, src, tgt, src_mass, tgt_mass, beta = call(
        functools.partial(first_kernel, dims, share_count),
        (
            shape(near_count, row_tiles, LANES),
            shape(depth, rows, dtype=BF16),
            shape(depth, cols, dtype=BF16),
            shape(row_tiles, LANES),
            shape(col_tiles, LANES),
            shape(col_tiles, LANES),
        ),
        [pltpu.VMEM((share_count, ROWS, own_cols), F32)],
    )(src_all, *tgts)
    row_all = swap(row_send, near)
    col_send, alpha, own_src = call(
        column_kernel,
        (shape(far_count, col_tiles, LANES), shape(row_tiles, LANES), shape(3 * ROWS, rows, dtype=BF16)),
        [pltpu.VMEM((col_tiles, LANES), F32)],
    )(row_all, src, src_mass, tgt, beta)
    col_all = swap(col_send, far)
    row_send, own_tgt, beta = call(
        row_kernel,
        (shape(near_count, row_tiles, LANES), shape(3 * ROWS, cols, dtype=BF16), shape(col_tiles, LANES)),
        [pltpu.VMEM((row_tiles, LANES), F32)],
    )(col_all, own_src, src, tgt, tgt_mass, alpha)
    row_all = swap(row_send, near)
    col_send, merged = call(
        functools.partial(last_column_kernel, share_count),
        (shape(far_count, own_cols // LANES, LANES), shape(row_tiles, LANES)),
        [pltpu.VMEM((3 * ROWS, rows), BF16), pltpu.VMEM((col_tiles, LANES), F32)],
    )(row_all, src, src_mass, own_tgt, tgt, beta)
    col_all = swap(col_send, far)
    row_potential, column_potential = call(
        functools.partial(final_kernel, near), (shape(1, own_rows), shape(own_cols // LANES, LANES))
    )(col_all, merged, sources, targets)
    return row_potential.reshape(own_rows), column_potential.reshape(own_cols)


def solution(mesh):
    split = Mesh(mesh.devices.reshape(8, 4, 4, 2), ("z", "y", "x", "c"))
    everywhere, column = ("z", "y", "x", "c"), ("y", "x", "c")
    return jax.shard_map(
        on_device,
        mesh=split,
        in_specs=(P(None, everywhere), P(everywhere), P(None, column), P(column), P(column)),
        out_specs=(P(everywhere), P(column)),
        check_vma=False,
    )
```

```python
import functools
import math

import jax
import jax.numpy as jnp
from jax import lax
from jax.experimental import pallas as pl
from jax.experimental.pallas import tpu as pltpu
from jax.sharding import Mesh, PartitionSpec as P


LOG2E = math.log2(math.e)
LN2 = math.log(2.0)
LANES = 128
TILE = 256
STEP = 128
PLAN_STEP = 512
SMALLEST = 2.0**-90
ROWS = 32
LEFT = (0, 0, 1, 1, 0, 2)
RIGHT = (0, 1, 0, 1, 2, 0)
F32, BF16 = jnp.float32, jnp.bfloat16


def parts_of(value):
    first = value.astype(BF16)
    rest = value - first.astype(F32)
    second = rest.astype(BF16)
    third = (rest - second.astype(F32)).astype(BF16)
    return first, second, third


def merge(values):
    peak = jnp.max(values, axis=0)
    return peak + LOG2E * jnp.log(jnp.sum(jnp.exp2(values - peak[None]), axis=0))


def row_of(shape, row):
    return lax.broadcasted_iota(jnp.int32, shape, 0) == row


def with_row(block, row, value):
    return jnp.where(row_of(block.shape, row), value, block)


def fold(left, count, right, width, step=STEP, tile=TILE):
    items = [(lane, at) for lane in range(0, width, tile) for at in range(0, count, step)]

    def scores_of(lane, at):
        return lax.dot_general(
            left(slice(at, at + step)),
            right(slice(lane, lane + tile)),
            (((0,), (0,)), ((), ())),
            preferred_element_type=F32,
        ).reshape(step // 8, 8, tile)

    lines = []
    coming = scores_of(*items[0])
    for number, (lane, at) in enumerate(items):
        scores = coming
        if number + 1 < len(items):
            coming = scores_of(*items[number + 1])
        if at == 0:
            peak = jnp.max(scores, axis=0)
            total = jnp.sum(jnp.exp2(scores - peak[None]), axis=0)
        else:
            new_peak = jnp.maximum(peak, jnp.max(scores, axis=0))
            total = total * jnp.exp2(peak - new_peak) + jnp.sum(jnp.exp2(scores - new_peak[None]), axis=0)
            peak = new_peak
        if at + step == count:
            top = jnp.max(peak, axis=0, keepdims=True)
            whole = jnp.sum(total * jnp.exp2(peak - top), axis=0, keepdims=True)
            lines.append(top + LOG2E * jnp.log(whole))
    return jnp.concatenate(lines, axis=1)


def plan_line(left, count, right, width, line_ref):
    lines = []
    for lane in range(0, width, TILE):
        total = jnp.zeros((8, TILE), F32)
        for at in range(0, count, PLAN_STEP):
            scores = lax.dot_general(
                left(slice(at, at + PLAN_STEP)),
                right(slice(lane, lane + TILE)),
                (((0,), (0,)), ((), ())),
                preferred_element_type=F32,
            ).reshape(PLAN_STEP // 8, 8, TILE)
            total = total + jnp.sum(jnp.exp2(scores), axis=0)
        lines.append(jnp.sum(total, axis=0, keepdims=True))
    set_rows(line_ref, jnp.concatenate(lines, axis=1), 0)
    sums = line_ref[...]
    line_ref[...] = LOG2E * jnp.log(sums)

    @pl.when(jnp.min(sums) < SMALLEST)
    def again():
        set_rows(line_ref, fold(left, count, right, width), 0)


def whole(ref):
    return lambda lanes: ref[:, lanes]


def patched(own_ref, ref):
    return lambda lanes: jnp.concatenate([own_ref[:, lanes], ref[own_ref.shape[0] :, lanes]], axis=0)


def as_rows(line):
    return [line[:, at : at + LANES] for at in range(0, line.shape[1], LANES)]


def set_rows(ref, line, row):
    for at, piece in enumerate(as_rows(line)):
        ref[row + at : row + at + 1, :] = piece


def pack_kernel(*refs):
    inputs, (src_out, tgt_out), held, sems = refs[:5], refs[5:7], refs[7:12], refs[12]
    copies = [
        pltpu.make_async_copy(whence, where, sems.at[at])
        for at, (whence, where) in enumerate(zip(inputs, held))
    ]
    for copy in copies:
        copy.start()
    for copy in copies:
        copy.wait()
    src, src_mass, tgt, tgt_mass, start = (ref[...] for ref in held)
    tgt_out[...] = jnp.concatenate([tgt, tgt_mass, start], axis=0)
    block = jnp.concatenate([src, src_mass, jnp.zeros((1, LANES), F32)], axis=0)
    src_out[...] = jnp.broadcast_to(block[None], src_out.shape)


def target_kernel(dims, share_count, *refs):
    tgt_refs = refs[:share_count]
    tgt_out, tgt_mass_out, beta_out, top_out, held = refs[share_count:]
    mine = lax.axis_index("c")
    for shift in range(share_count):
        held[lax.rem(mine + share_count - shift, share_count)] = tgt_refs[shift][...]
    width = held.shape[2]
    top = None
    for group in range(share_count):
        block = held[group]
        mass = LOG2E * block[dims : dims + 1, :]
        set_rows(tgt_mass_out, mass, group * (width // LANES))
        spare = lax.broadcasted_iota(jnp.int32, block.shape, 0) >= dims
        coords = jnp.where(spare, 0.0, block)
        split = parts_of(coords)
        norm = jnp.sum(coords * coords, axis=0, keepdims=True)
        term = mass + (0.5 * LOG2E) * block[dims + 1 : dims + 2, :]
        highest = jnp.max(term, axis=1, keepdims=True)
        top = highest if top is None else jnp.maximum(top, highest)
        beta = term - (0.25 * LOG2E) * norm
        set_rows(beta_out, beta, group * (width // LANES))
        beta_parts = parts_of(beta)
        lanes = slice(group * width, group * width + width)
        for slot, which in enumerate(RIGHT):
            piece = split[which].astype(F32)
            if slot < 3:
                piece = with_row(piece, ROWS - 2, beta_parts[slot].astype(F32))
                piece = with_row(piece, ROWS - 1, 1.0)
            tgt_out[slot * ROWS : slot * ROWS + ROWS, lanes] = piece.astype(BF16)
    top_out[...] = jnp.broadcast_to(top, top_out.shape)


def first_kernel(dims, src_ref, tgt_ref, top_ref, row_out, src_out, src_mass_out, alpha_ref, line_ref):
    for group in range(src_ref.shape[0]):
        block = src_ref[group]
        src_mass_out[group : group + 1, :] = LOG2E * block[dims : dims + 1, :]
        spare = lax.broadcasted_iota(jnp.int32, block.shape, 0) >= dims
        coords = jnp.where(spare, 0.0, block)
        split = parts_of((0.5 * LOG2E) * coords)
        alpha = (-0.25 * LOG2E) * jnp.sum(coords * coords, axis=0, keepdims=True) - top_ref[...]
        alpha_ref[group : group + 1, :] = alpha
        alpha_parts = parts_of(alpha)
        lanes = slice(group * LANES, group * LANES + LANES)
        for slot, which in enumerate(LEFT):
            piece = split[which].astype(F32)
            if slot < 3:
                piece = with_row(piece, ROWS - 2, 1.0)
                piece = with_row(piece, ROWS - 1, alpha_parts[slot].astype(F32))
            src_out[slot * ROWS : slot * ROWS + ROWS, lanes] = piece.astype(BF16)
    plan_line(whole(tgt_ref), tgt_ref.shape[1], whole(src_out), src_out.shape[1], line_ref)
    row_out[...] = jnp.broadcast_to((line_ref[...] - alpha_ref[...])[None], row_out.shape)


def set_terms(own_ref, ref, values, row):
    split = parts_of(values)
    for group in range(values.shape[0]):
        lanes = slice(group * LANES, group * LANES + LANES)
        for slot in range(3):
            rows = slice(slot * ROWS, slot * ROWS + ROWS)
            block = ref[rows, lanes].astype(F32)
            own_ref[rows, lanes] = with_row(block, row, split[slot][group : group + 1, :].astype(F32)).astype(BF16)


def column_kernel(rows_ref, src_ref, src_mass_ref, tgt_ref, beta_ref, col_out, alpha_out, own_src, line_ref):
    alpha = src_mass_ref[...] - merge(rows_ref[...])
    alpha_out[...] = alpha
    set_terms(own_src, src_ref, alpha, ROWS - 1)
    plan_line(patched(own_src, src_ref), src_ref.shape[1], whole(tgt_ref), tgt_ref.shape[1], line_ref)
    col_out[...] = jnp.broadcast_to((line_ref[...] - beta_ref[...])[None], col_out.shape)


def row_kernel(
    cols_ref, own_src, src_ref, tgt_ref, tgt_mass_ref, alpha_ref, row_out, own_tgt, beta_out, line_ref
):
    beta = tgt_mass_ref[...] - merge(cols_ref[...])
    beta_out[...] = beta
    set_terms(own_tgt, tgt_ref, beta, ROWS - 2)
    plan_line(
        patched(own_tgt, tgt_ref), tgt_ref.shape[1], patched(own_src, src_ref), src_ref.shape[1], line_ref
    )
    row_out[...] = jnp.broadcast_to((line_ref[...] - alpha_ref[...])[None], row_out.shape)


def last_column_kernel(
    share_count, rows_ref, src_ref, src_mass_ref, own_tgt, tgt_ref, beta_ref, col_out, merged_out, own_src, line_ref
):
    merged = merge(rows_ref[...])
    merged_out[...] = merged
    set_terms(own_src, src_ref, src_mass_ref[...] - merged, ROWS - 1)
    plan_line(
        patched(own_src, src_ref), src_ref.shape[1], patched(own_tgt, tgt_ref), tgt_ref.shape[1], line_ref
    )
    line = line_ref[...] - beta_ref[...]
    share = line.shape[0] // share_count
    for part in range(share_count):
        for to in range(part, col_out.shape[0], share_count):
            col_out[to] = line[part * share : part * share + share]


def final_kernel(near, cols_ref, rows_ref, src_ref, tgt_ref, row_out, pot_out):
    mine = rows_ref[pl.ds(lax.axis_index(near), 1), :]
    coords = src_ref[...]
    norm = jnp.sum(coords * coords, axis=0, keepdims=True)
    row_out[...] = 0.5 * norm - (2.0 * LN2) * mine
    merged = merge(cols_ref[...])
    coords = tgt_ref[...]
    norm = jnp.sum(coords * coords, axis=0, keepdims=True)
    for at, piece in enumerate(as_rows(norm)):
        pot_out[at : at + 1, :] = 0.5 * piece - (2.0 * LN2) * merged[at : at + 1, :]


def call(kernel, outs, scratch=(), mib=24, **more):
    return pl.pallas_call(
        kernel,
        out_shape=outs,
        **more,
        scratch_shapes=list(scratch),
        compiler_params=pltpu.CompilerParams(vmem_limit_bytes=mib * 1024 * 1024),
    )


def shape(*dims, dtype=F32):
    return jax.ShapeDtypeStruct(dims, dtype)


def on_device(sources, log_source_mass, targets, log_target_mass, start_potential):
    near, far = ("y", "x"), ("z", "c")
    dims, own_rows = sources.shape
    own_cols = targets.shape[1]
    near_count, share_count = lax.axis_size(near), lax.axis_size("c")
    far_count = lax.axis_size(far)
    rows, cols = near_count * own_rows, share_count * own_cols
    row_tiles, col_tiles = rows // LANES, cols // LANES
    depth = len(LEFT) * ROWS

    def swap(value, axes):
        return lax.all_to_all(value, axes, 0, 0, tiled=True)

    given = (sources, log_source_mass[None], targets, log_target_mass[None], start_potential[None])
    src_send, tgt_own = call(
        pack_kernel,
        (shape(near_count, ROWS, LANES), shape(ROWS, own_cols)),
        [pltpu.VMEM(array.shape, F32) for array in given] + [pltpu.SemaphoreType.DMA((len(given),))],
        in_specs=[pl.BlockSpec(memory_space=pl.ANY)] * len(given),
    )(*[pltpu.with_memory_space_constraint(array, pltpu.HBM) for array in given])
    tgts = [tgt_own] + [
        lax.ppermute(tgt_own, "c", [(k, (k + shift) % share_count) for k in range(share_count)])
        for shift in range(1, share_count)
    ]
    src_all = swap(src_send, near)
    tgt, tgt_mass, beta, top = call(
        functools.partial(target_kernel, dims, share_count),
        (
            shape(depth, cols, dtype=BF16),
            shape(col_tiles, LANES),
            shape(col_tiles, LANES),
            shape(1, LANES),
        ),
        [pltpu.VMEM((share_count, ROWS, own_cols), F32)],
    )(*tgts)
    row_send, src, src_mass = call(
        functools.partial(first_kernel, dims),
        (
            shape(near_count, row_tiles, LANES),
            shape(depth, rows, dtype=BF16),
            shape(row_tiles, LANES),
        ),
        [pltpu.VMEM((row_tiles, LANES), F32)] * 2,
    )(src_all, tgt, top)
    row_all = swap(row_send, near)
    col_send, alpha, own_src = call(
        column_kernel,
        (shape(far_count, col_tiles, LANES), shape(row_tiles, LANES), shape(3 * ROWS, rows, dtype=BF16)),
        [pltpu.VMEM((col_tiles, LANES), F32)],
    )(row_all, src, src_mass, tgt, beta)
    col_all = swap(col_send, far)
    row_send, own_tgt, beta = call(
        row_kernel,
        (shape(near_count, row_tiles, LANES), shape(3 * ROWS, cols, dtype=BF16), shape(col_tiles, LANES)),
        [pltpu.VMEM((row_tiles, LANES), F32)],
    )(col_all, own_src, src, tgt, tgt_mass, alpha)
    row_all = swap(row_send, near)
    col_send, merged = call(
        functools.partial(last_column_kernel, share_count),
        (shape(far_count, own_cols // LANES, LANES), shape(row_tiles, LANES)),
        [pltpu.VMEM((3 * ROWS, rows), BF16), pltpu.VMEM((col_tiles, LANES), F32)],
    )(row_all, src, src_mass, own_tgt, tgt, beta)
    col_all = swap(col_send, far)
    row_potential, column_potential = call(
        functools.partial(final_kernel, near), (shape(1, own_rows), shape(own_cols // LANES, LANES))
    )(col_all, merged, sources, targets)
    return row_potential.reshape(own_rows), column_potential.reshape(own_cols)


def solution(mesh):
    split = Mesh(mesh.devices.reshape(8, 4, 4, 2), ("z", "y", "x", "c"))
    everywhere, column = ("z", "y", "x", "c"), ("y", "x", "c")
    return jax.shard_map(
        on_device,
        mesh=split,
        in_specs=(P(None, everywhere), P(everywhere), P(None, column), P(column), P(column)),
        out_specs=(P(everywhere), P(column)),
        check_vma=False,
    )
```

```python
import functools
import math

import jax
import jax.numpy as jnp
from jax import lax
from jax.experimental import pallas as pl
from jax.experimental.pallas import tpu as pltpu
from jax.sharding import Mesh, PartitionSpec as P


LOG2E = math.log2(math.e)
LN2 = math.log(2.0)
LANES = 128
TILE = 256
STEP = 128
PLAN_STEP = 512
SMALLEST = 2.0**-90
ROWS = 32
LEFT = (0, 0, 1, 1, 0, 2)
RIGHT = (0, 1, 0, 1, 2, 0)
F32, BF16 = jnp.float32, jnp.bfloat16


def parts_of(value):
    first = value.astype(BF16)
    rest = value - first.astype(F32)
    second = rest.astype(BF16)
    third = (rest - second.astype(F32)).astype(BF16)
    return first, second, third


def merge(values):
    peak = jnp.max(values, axis=0)
    return peak + LOG2E * jnp.log(jnp.sum(jnp.exp2(values - peak[None]), axis=0))


def row_of(shape, row):
    return lax.broadcasted_iota(jnp.int32, shape, 0) == row


def with_row(block, row, value):
    return jnp.where(row_of(block.shape, row), value, block)


def fold(left, count, right, width, step=STEP, tile=TILE):
    items = [(lane, at) for lane in range(0, width, tile) for at in range(0, count, step)]

    def scores_of(lane, at):
        return lax.dot_general(
            left(slice(at, at + step)),
            right(slice(lane, lane + tile)),
            (((0,), (0,)), ((), ())),
            preferred_element_type=F32,
        ).reshape(step // 8, 8, tile)

    lines = []
    coming = scores_of(*items[0])
    for number, (lane, at) in enumerate(items):
        scores = coming
        if number + 1 < len(items):
            coming = scores_of(*items[number + 1])
        if at == 0:
            peak = jnp.max(scores, axis=0)
            total = jnp.sum(jnp.exp2(scores - peak[None]), axis=0)
        else:
            new_peak = jnp.maximum(peak, jnp.max(scores, axis=0))
            total = total * jnp.exp2(peak - new_peak) + jnp.sum(jnp.exp2(scores - new_peak[None]), axis=0)
            peak = new_peak
        if at + step == count:
            top = jnp.max(peak, axis=0, keepdims=True)
            whole = jnp.sum(total * jnp.exp2(peak - top), axis=0, keepdims=True)
            lines.append(top + LOG2E * jnp.log(whole))
    return jnp.concatenate(lines, axis=1)


def plan_line(left, count, right, width, line_ref):
    lines = []
    for lane in range(0, width, TILE):
        total = jnp.zeros((8, TILE), F32)
        for at in range(0, count, PLAN_STEP):
            scores = lax.dot_general(
                left(slice(at, at + PLAN_STEP)),
                right(slice(lane, lane + TILE)),
                (((0,), (0,)), ((), ())),
                preferred_element_type=F32,
            ).reshape(PLAN_STEP // 8, 8, TILE)
            total = total + jnp.sum(jnp.exp2(scores), axis=0)
        lines.append(jnp.sum(total, axis=0, keepdims=True))
    set_rows(line_ref, jnp.concatenate(lines, axis=1), 0)
    sums = line_ref[...]
    line_ref[...] = LOG2E * jnp.log(sums)

    @pl.when(jnp.min(sums) < SMALLEST)
    def again():
        set_rows(line_ref, fold(left, count, right, width), 0)


def whole(ref):
    return lambda lanes: ref[:, lanes]


def patched(own_ref, ref):
    return lambda lanes: jnp.concatenate([own_ref[:, lanes], ref[own_ref.shape[0] :, lanes]], axis=0)


def as_rows(line):
    return [line[:, at : at + LANES] for at in range(0, line.shape[1], LANES)]


def set_rows(ref, line, row):
    for at, piece in enumerate(as_rows(line)):
        ref[row + at : row + at + 1, :] = piece


def pack_kernel(copies_out, spare_rows, *refs):
    count = len(refs) // 2 - 1
    inputs, out, held, sems = refs[:count], refs[count], refs[count + 1 : -1], refs[-1]
    copies = [
        pltpu.make_async_copy(whence, where, sems.at[at])
        for at, (whence, where) in enumerate(zip(inputs, held))
    ]
    for copy in copies:
        copy.start()
    for copy in copies:
        copy.wait()
    rows = [ref[...] for ref in held]
    if spare_rows:
        rows.append(jnp.zeros((spare_rows, rows[0].shape[1]), F32))
    block = jnp.concatenate(rows, axis=0)
    out[...] = jnp.broadcast_to(block[None], out.shape) if copies_out else block


def pack(given, out):
    copies_out = len(out.shape) == 3
    spare_rows = ROWS - sum(array.shape[0] for array in given)
    return call(
        functools.partial(pack_kernel, copies_out, spare_rows),
        out,
        [pltpu.VMEM(array.shape, F32) for array in given] + [pltpu.SemaphoreType.DMA((len(given),))],
        in_specs=[pl.BlockSpec(memory_space=pl.ANY)] * len(given),
    )(*[pltpu.with_memory_space_constraint(array, pltpu.HBM) for array in given])


def target_kernel(dims, share_count, *refs):
    tgt_refs = refs[:share_count]
    tgt_out, tgt_mass_out, beta_out, top_out, held = refs[share_count:]
    mine = lax.axis_index("c")
    for shift in range(share_count):
        held[lax.rem(mine + share_count - shift, share_count)] = tgt_refs[shift][...]
    width = held.shape[2]
    top = None
    for group in range(share_count):
        block = held[group]
        mass = LOG2E * block[dims : dims + 1, :]
        set_rows(tgt_mass_out, mass, group * (width // LANES))
        spare = lax.broadcasted_iota(jnp.int32, block.shape, 0) >= dims
        coords = jnp.where(spare, 0.0, block)
        split = parts_of(coords)
        norm = jnp.sum(coords * coords, axis=0, keepdims=True)
        term = mass + (0.5 * LOG2E) * block[dims + 1 : dims + 2, :]
        highest = jnp.max(term, axis=1, keepdims=True)
        top = highest if top is None else jnp.maximum(top, highest)
        beta = term - (0.25 * LOG2E) * norm
        set_rows(beta_out, beta, group * (width // LANES))
        beta_parts = parts_of(beta)
        lanes = slice(group * width, group * width + width)
        for slot, which in enumerate(RIGHT):
            piece = split[which].astype(F32)
            if slot < 3:
                piece = with_row(piece, ROWS - 2, beta_parts[slot].astype(F32))
                piece = with_row(piece, ROWS - 1, 1.0)
            tgt_out[slot * ROWS : slot * ROWS + ROWS, lanes] = piece.astype(BF16)
    top_out[...] = jnp.broadcast_to(top, top_out.shape)


def first_kernel(dims, src_ref, tgt_ref, top_ref, row_out, src_out, src_mass_out, alpha_ref, line_ref):
    for group in range(src_ref.shape[0]):
        block = src_ref[group]
        src_mass_out[group : group + 1, :] = LOG2E * block[dims : dims + 1, :]
        spare = lax.broadcasted_iota(jnp.int32, block.shape, 0) >= dims
        coords = jnp.where(spare, 0.0, block)
        split = parts_of((0.5 * LOG2E) * coords)
        alpha = (-0.25 * LOG2E) * jnp.sum(coords * coords, axis=0, keepdims=True) - top_ref[...]
        alpha_ref[group : group + 1, :] = alpha
        alpha_parts = parts_of(alpha)
        lanes = slice(group * LANES, group * LANES + LANES)
        for slot, which in enumerate(LEFT):
            piece = split[which].astype(F32)
            if slot < 3:
                piece = with_row(piece, ROWS - 2, 1.0)
                piece = with_row(piece, ROWS - 1, alpha_parts[slot].astype(F32))
            src_out[slot * ROWS : slot * ROWS + ROWS, lanes] = piece.astype(BF16)
    plan_line(whole(tgt_ref), tgt_ref.shape[1], whole(src_out), src_out.shape[1], line_ref)
    row_out[...] = jnp.broadcast_to((line_ref[...] - alpha_ref[...])[None], row_out.shape)


def set_terms(own_ref, ref, values, row):
    split = parts_of(values)
    for group in range(values.shape[0]):
        lanes = slice(group * LANES, group * LANES + LANES)
        for slot in range(3):
            rows = slice(slot * ROWS, slot * ROWS + ROWS)
            block = ref[rows, lanes].astype(F32)
            own_ref[rows, lanes] = with_row(block, row, split[slot][group : group + 1, :].astype(F32)).astype(BF16)


def column_kernel(rows_ref, src_ref, src_mass_ref, tgt_ref, beta_ref, col_out, alpha_out, own_src, line_ref):
    alpha = src_mass_ref[...] - merge(rows_ref[...])
    alpha_out[...] = alpha
    set_terms(own_src, src_ref, alpha, ROWS - 1)
    plan_line(patched(own_src, src_ref), src_ref.shape[1], whole(tgt_ref), tgt_ref.shape[1], line_ref)
    col_out[...] = jnp.broadcast_to((line_ref[...] - beta_ref[...])[None], col_out.shape)


def row_kernel(
    cols_ref, own_src, src_ref, tgt_ref, tgt_mass_ref, alpha_ref, row_out, own_tgt, beta_out, line_ref
):
    beta = tgt_mass_ref[...] - merge(cols_ref[...])
    beta_out[...] = beta
    set_terms(own_tgt, tgt_ref, beta, ROWS - 2)
    plan_line(
        patched(own_tgt, tgt_ref), tgt_ref.shape[1], patched(own_src, src_ref), src_ref.shape[1], line_ref
    )
    row_out[...] = jnp.broadcast_to((line_ref[...] - alpha_ref[...])[None], row_out.shape)


def last_column_kernel(
    share_count, rows_ref, src_ref, src_mass_ref, own_tgt, tgt_ref, beta_ref, col_out, merged_out, own_src, line_ref
):
    merged = merge(rows_ref[...])
    merged_out[...] = merged
    set_terms(own_src, src_ref, src_mass_ref[...] - merged, ROWS - 1)
    plan_line(
        patched(own_src, src_ref), src_ref.shape[1], patched(own_tgt, tgt_ref), tgt_ref.shape[1], line_ref
    )
    line = line_ref[...] - beta_ref[...]
    share = line.shape[0] // share_count
    for part in range(share_count):
        for to in range(part, col_out.shape[0], share_count):
            col_out[to] = line[part * share : part * share + share]


def final_kernel(near, cols_ref, rows_ref, src_ref, tgt_ref, row_out, pot_out):
    mine = rows_ref[pl.ds(lax.axis_index(near), 1), :]
    coords = src_ref[...]
    norm = jnp.sum(coords * coords, axis=0, keepdims=True)
    row_out[...] = 0.5 * norm - (2.0 * LN2) * mine
    merged = merge(cols_ref[...])
    coords = tgt_ref[...]
    norm = jnp.sum(coords * coords, axis=0, keepdims=True)
    for at, piece in enumerate(as_rows(norm)):
        pot_out[at : at + 1, :] = 0.5 * piece - (2.0 * LN2) * merged[at : at + 1, :]


def call(kernel, outs, scratch=(), mib=24, **more):
    return pl.pallas_call(
        kernel,
        out_shape=outs,
        **more,
        scratch_shapes=list(scratch),
        compiler_params=pltpu.CompilerParams(vmem_limit_bytes=mib * 1024 * 1024),
    )


def shape(*dims, dtype=F32):
    return jax.ShapeDtypeStruct(dims, dtype)


def on_device(sources, log_source_mass, targets, log_target_mass, start_potential):
    near, far = ("y", "x"), ("z", "c")
    dims, own_rows = sources.shape
    own_cols = targets.shape[1]
    near_count, share_count = lax.axis_size(near), lax.axis_size("c")
    far_count = lax.axis_size(far)
    rows, cols = near_count * own_rows, share_count * own_cols
    row_tiles, col_tiles = rows // LANES, cols // LANES
    depth = len(LEFT) * ROWS

    def swap(value, axes):
        return lax.all_to_all(value, axes, 0, 0, tiled=True)

    src_send = pack((sources, log_source_mass[None]), shape(near_count, ROWS, LANES))
    src_all = swap(src_send, near)
    tgt_own = pack((targets, log_target_mass[None], start_potential[None]), shape(ROWS, own_cols))
    tgts = [tgt_own] + [
        lax.ppermute(tgt_own, "c", [(k, (k + shift) % share_count) for k in range(share_count)])
        for shift in range(1, share_count)
    ]
    tgt, tgt_mass, beta, top = call(
        functools.partial(target_kernel, dims, share_count),
        (
            shape(depth, cols, dtype=BF16),
            shape(col_tiles, LANES),
            shape(col_tiles, LANES),
            shape(1, LANES),
        ),
        [pltpu.VMEM((share_count, ROWS, own_cols), F32)],
    )(*tgts)
    row_send, src, src_mass = call(
        functools.partial(first_kernel, dims),
        (
            shape(near_count, row_tiles, LANES),
            shape(depth, rows, dtype=BF16),
            shape(row_tiles, LANES),
        ),
        [pltpu.VMEM((row_tiles, LANES), F32)] * 2,
    )(src_all, tgt, top)
    row_all = swap(row_send, near)
    col_send, alpha, own_src = call(
        column_kernel,
        (shape(far_count, col_tiles, LANES), shape(row_tiles, LANES), shape(3 * ROWS, rows, dtype=BF16)),
        [pltpu.VMEM((col_tiles, LANES), F32)],
    )(row_all, src, src_mass, tgt, beta)
    col_all = swap(col_send, far)
    row_send, own_tgt, beta = call(
        row_kernel,
        (shape(near_count, row_tiles, LANES), shape(3 * ROWS, cols, dtype=BF16), shape(col_tiles, LANES)),
        [pltpu.VMEM((row_tiles, LANES), F32)],
    )(col_all, own_src, src, tgt, tgt_mass, alpha)
    row_all = swap(row_send, near)
    col_send, merged = call(
        functools.partial(last_column_kernel, share_count),
        (shape(far_count, own_cols // LANES, LANES), shape(row_tiles, LANES)),
        [pltpu.VMEM((3 * ROWS, rows), BF16), pltpu.VMEM((col_tiles, LANES), F32)],
    )(row_all, src, src_mass, own_tgt, tgt, beta)
    col_all = swap(col_send, far)
    row_potential, column_potential = call(
        functools.partial(final_kernel, near), (shape(1, own_rows), shape(own_cols // LANES, LANES))
    )(col_all, merged, sources, targets)
    return row_potential.reshape(own_rows), column_potential.reshape(own_cols)


def solution(mesh):
    split = Mesh(mesh.devices.reshape(8, 4, 4, 2), ("z", "y", "x", "c"))
    everywhere, column = ("z", "y", "x", "c"), ("y", "x", "c")
    return jax.shard_map(
        on_device,
        mesh=split,
        in_specs=(P(None, everywhere), P(everywhere), P(None, column), P(column), P(column)),
        out_specs=(P(everywhere), P(column)),
        check_vma=False,
    )
```

```python
import functools
import math

import jax
import jax.numpy as jnp
from jax import lax
from jax.experimental import pallas as pl
from jax.experimental.pallas import tpu as pltpu
from jax.sharding import Mesh, PartitionSpec as P


LOG2E = math.log2(math.e)
LN2 = math.log(2.0)
LANES = 128
TILE = 256
STEP = 128
PLAN_STEP = 256
SMALLEST = 2.0**-90
LARGEST = 2.0**100
ROWS = 32
LEFT = (0, 0, 1, 1, 0, 2)
RIGHT = (0, 1, 0, 1, 2, 0)
F32, BF16 = jnp.float32, jnp.bfloat16


def parts_of(value):
    first = value.astype(BF16)
    rest = value - first.astype(F32)
    second = rest.astype(BF16)
    third = (rest - second.astype(F32)).astype(BF16)
    return first, second, third


def merge(values):
    peak = jnp.max(values, axis=0)
    return peak + LOG2E * jnp.log(jnp.sum(jnp.exp2(values - peak[None]), axis=0))


def row_of(shape, row):
    return lax.broadcasted_iota(jnp.int32, shape, 0) == row


def with_row(block, row, value):
    return jnp.where(row_of(block.shape, row), value, block)


def fold(left, count, right, width, step=STEP, tile=TILE):
    items = [(lane, at) for lane in range(0, width, tile) for at in range(0, count, step)]

    def scores_of(lane, at):
        return lax.dot_general(
            left(slice(at, at + step)),
            right(slice(lane, lane + tile)),
            (((0,), (0,)), ((), ())),
            preferred_element_type=F32,
        ).reshape(step // 8, 8, tile)

    lines = []
    coming = scores_of(*items[0])
    for number, (lane, at) in enumerate(items):
        scores = coming
        if number + 1 < len(items):
            coming = scores_of(*items[number + 1])
        if at == 0:
            peak = jnp.max(scores, axis=0)
            total = jnp.sum(jnp.exp2(scores - peak[None]), axis=0)
        else:
            new_peak = jnp.maximum(peak, jnp.max(scores, axis=0))
            total = total * jnp.exp2(peak - new_peak) + jnp.sum(jnp.exp2(scores - new_peak[None]), axis=0)
            peak = new_peak
        if at + step == count:
            top = jnp.max(peak, axis=0, keepdims=True)
            whole = jnp.sum(total * jnp.exp2(peak - top), axis=0, keepdims=True)
            lines.append(top + LOG2E * jnp.log(whole))
    return jnp.concatenate(lines, axis=1)


def plan_line(left, count, right, width, line_ref, kept_ref):
    spots = range(0, width, TILE)
    totals = [jnp.zeros((8, TILE), F32) for lane in spots]
    for at in range(0, count, PLAN_STEP):
        block = left(slice(at, at + PLAN_STEP))
        for number, lane in enumerate(spots):
            scores = lax.dot_general(
                block, right(slice(lane, lane + TILE)), (((0,), (0,)), ((), ())), preferred_element_type=F32
            )
            terms = jnp.exp2(scores)
            kept_ref[at : at + PLAN_STEP, lane : lane + TILE] = terms
            totals[number] = totals[number] + jnp.sum(terms.reshape(PLAN_STEP // 8, 8, TILE), axis=0)
    lines = [jnp.sum(total, axis=0, keepdims=True) for total in totals]
    set_rows(line_ref, jnp.concatenate(lines, axis=1), 0)
    sums = line_ref[...]
    line_ref[...] = LOG2E * jnp.log(sums)

    @pl.when(jnp.min(sums) < SMALLEST)
    def again():
        set_rows(line_ref, fold(left, count, right, width), 0)


def whole(ref):
    return lambda lanes: ref[:, lanes]


def patched(own_ref, ref):
    return lambda lanes: jnp.concatenate([own_ref[:, lanes], ref[own_ref.shape[0] :, lanes]], axis=0)


def as_rows(line):
    return [line[:, at : at + LANES] for at in range(0, line.shape[1], LANES)]


def set_rows(ref, line, row):
    for at, piece in enumerate(as_rows(line)):
        ref[row + at : row + at + 1, :] = piece


def pack_kernel(copies_out, spare_rows, *refs):
    count = len(refs) // 2 - 1
    inputs, out, held, sems = refs[:count], refs[count], refs[count + 1 : -1], refs[-1]
    copies = [
        pltpu.make_async_copy(whence, where, sems.at[at])
        for at, (whence, where) in enumerate(zip(inputs, held))
    ]
    for copy in copies:
        copy.start()
    for copy in copies:
        copy.wait()
    rows = [ref[...] for ref in held]
    if spare_rows:
        rows.append(jnp.zeros((spare_rows, rows[0].shape[1]), F32))
    block = jnp.concatenate(rows, axis=0)
    out[...] = jnp.broadcast_to(block[None], out.shape) if copies_out else block


def pack(given, out):
    copies_out = len(out.shape) == 3
    spare_rows = ROWS - sum(array.shape[0] for array in given)
    return call(
        functools.partial(pack_kernel, copies_out, spare_rows),
        out,
        [pltpu.VMEM(array.shape, F32) for array in given] + [pltpu.SemaphoreType.DMA((len(given),))],
        in_specs=[pl.BlockSpec(memory_space=pl.ANY)] * len(given),
    )(*[pltpu.with_memory_space_constraint(array, pltpu.HBM) for array in given])


def target_kernel(dims, share_count, *refs):
    tgt_refs = refs[:share_count]
    tgt_out, tgt_mass_out, beta_out, top_out, held = refs[share_count:]
    mine = lax.axis_index("c")
    for shift in range(share_count):
        held[lax.rem(mine + share_count - shift, share_count)] = tgt_refs[shift][...]
    width = held.shape[2]
    top = None
    for group in range(share_count):
        block = held[group]
        mass = LOG2E * block[dims : dims + 1, :]
        set_rows(tgt_mass_out, mass, group * (width // LANES))
        spare = lax.broadcasted_iota(jnp.int32, block.shape, 0) >= dims
        coords = jnp.where(spare, 0.0, block)
        split = parts_of(coords)
        norm = jnp.sum(coords * coords, axis=0, keepdims=True)
        term = mass + (0.5 * LOG2E) * block[dims + 1 : dims + 2, :]
        highest = jnp.max(term, axis=1, keepdims=True)
        top = highest if top is None else jnp.maximum(top, highest)
        beta = term - (0.25 * LOG2E) * norm
        set_rows(beta_out, beta, group * (width // LANES))
        beta_parts = parts_of(beta)
        lanes = slice(group * width, group * width + width)
        for slot, which in enumerate(RIGHT):
            piece = split[which].astype(F32)
            if slot < 3:
                piece = with_row(piece, ROWS - 2, beta_parts[slot].astype(F32))
                piece = with_row(piece, ROWS - 1, 1.0)
            tgt_out[slot * ROWS : slot * ROWS + ROWS, lanes] = piece.astype(BF16)
    top_out[...] = jnp.broadcast_to(top, top_out.shape)


def first_kernel(dims, src_ref, tgt_ref, top_ref, row_out, src_out, src_mass_out, alpha_ref, kept_ref, line_ref):
    for group in range(src_ref.shape[0]):
        block = src_ref[group]
        src_mass_out[group : group + 1, :] = LOG2E * block[dims : dims + 1, :]
        spare = lax.broadcasted_iota(jnp.int32, block.shape, 0) >= dims
        coords = jnp.where(spare, 0.0, block)
        split = parts_of((0.5 * LOG2E) * coords)
        alpha = (-0.25 * LOG2E) * jnp.sum(coords * coords, axis=0, keepdims=True) - top_ref[...]
        alpha_ref[group : group + 1, :] = alpha
        alpha_parts = parts_of(alpha)
        lanes = slice(group * LANES, group * LANES + LANES)
        for slot, which in enumerate(LEFT):
            piece = split[which].astype(F32)
            if slot < 3:
                piece = with_row(piece, ROWS - 2, 1.0)
                piece = with_row(piece, ROWS - 1, alpha_parts[slot].astype(F32))
            src_out[slot * ROWS : slot * ROWS + ROWS, lanes] = piece.astype(BF16)
    plan_line(whole(tgt_ref), tgt_ref.shape[1], whole(src_out), src_out.shape[1], line_ref, kept_ref)
    row_out[...] = jnp.broadcast_to((line_ref[...] - alpha_ref[...])[None], row_out.shape)


def set_terms(own_ref, ref, values, row):
    split = parts_of(values)
    for group in range(values.shape[0]):
        lanes = slice(group * LANES, group * LANES + LANES)
        for slot in range(3):
            rows = slice(slot * ROWS, slot * ROWS + ROWS)
            block = ref[rows, lanes].astype(F32)
            own_ref[rows, lanes] = with_row(block, row, split[slot][group : group + 1, :].astype(F32)).astype(BF16)


def too_small(sums, weights):
    most = jnp.maximum(jnp.max(weights), 1.0)
    return (jnp.min(sums) < SMALLEST * most) | (most > LARGEST)


def column_line(merged, kept_ref, src_ref, src_mass_ref, alpha_ref, tgt_ref, own_src, line_ref):
    alpha = src_mass_ref[...] - merged
    weights = jnp.exp2(alpha - alpha_ref[...])
    rows, tiles = line_ref.shape[0], weights.shape[0]
    for group in range(rows):
        block = slice(group * LANES, group * LANES + LANES)
        total = kept_ref[block, 0:LANES] * weights[0:1, :]
        for tile in range(1, tiles):
            total = total + kept_ref[block, tile * LANES : tile * LANES + LANES] * weights[tile : tile + 1, :]
        line_ref[group : group + 1, :] = jnp.sum(total.T, axis=0, keepdims=True)
    sums = line_ref[...]
    line_ref[...] = LOG2E * jnp.log(sums)

    @pl.when(too_small(sums, weights))
    def again():
        set_terms(own_src, src_ref, alpha, ROWS - 1)
        line = fold(patched(own_src, src_ref), src_ref.shape[1], whole(tgt_ref), tgt_ref.shape[1])
        set_rows(line_ref, line, 0)


def column_kernel(
    rows_ref, kept_ref, src_ref, src_mass_ref, alpha_ref, tgt_ref, beta_ref, col_out, own_src, line_ref
):
    column_line(merge(rows_ref[...]), kept_ref, src_ref, src_mass_ref, alpha_ref, tgt_ref, own_src, line_ref)
    col_out[...] = jnp.broadcast_to((line_ref[...] - beta_ref[...])[None], col_out.shape)


def row_kernel(
    cols_ref, kept_ref, src_ref, tgt_ref, tgt_mass_ref, beta_ref, alpha_ref, row_out, own_tgt, line_ref
):
    beta = tgt_mass_ref[...] - merge(cols_ref[...])
    weights = jnp.exp2(beta - beta_ref[...])
    columns = jnp.concatenate([weights, jnp.zeros((LANES - weights.shape[0], LANES), F32)], axis=0).T
    total = jnp.zeros((8, kept_ref.shape[1]), F32)
    for group in range(weights.shape[0]):
        for at in range(0, LANES, 8):
            weight = jnp.broadcast_to(columns[at : at + 8, group : group + 1], total.shape)
            total = total + kept_ref[group * LANES + at : group * LANES + at + 8, :] * weight
    set_rows(line_ref, jnp.sum(total, axis=0, keepdims=True), 0)
    sums = line_ref[...]
    line_ref[...] = LOG2E * jnp.log(sums)

    @pl.when(too_small(sums, weights))
    def again():
        set_terms(own_tgt, tgt_ref, beta, ROWS - 2)
        line = fold(patched(own_tgt, tgt_ref), tgt_ref.shape[1], whole(src_ref), src_ref.shape[1])
        set_rows(line_ref, line, 0)

    row_out[...] = jnp.broadcast_to((line_ref[...] - alpha_ref[...])[None], row_out.shape)


def last_column_kernel(
    share_count,
    rows_ref,
    kept_ref,
    src_ref,
    src_mass_ref,
    alpha_ref,
    tgt_ref,
    beta_ref,
    col_out,
    merged_out,
    own_src,
    line_ref,
):
    merged = merge(rows_ref[...])
    merged_out[...] = merged
    column_line(merged, kept_ref, src_ref, src_mass_ref, alpha_ref, tgt_ref, own_src, line_ref)
    line = line_ref[...] - beta_ref[...]
    share = line.shape[0] // share_count
    for part in range(share_count):
        for to in range(part, col_out.shape[0], share_count):
            col_out[to] = line[part * share : part * share + share]


def final_kernel(near, cols_ref, rows_ref, src_ref, tgt_ref, row_out, pot_out):
    mine = rows_ref[pl.ds(lax.axis_index(near), 1), :]
    coords = src_ref[...]
    norm = jnp.sum(coords * coords, axis=0, keepdims=True)
    row_out[...] = 0.5 * norm - (2.0 * LN2) * mine
    merged = merge(cols_ref[...])
    coords = tgt_ref[...]
    norm = jnp.sum(coords * coords, axis=0, keepdims=True)
    for at, piece in enumerate(as_rows(norm)):
        pot_out[at : at + 1, :] = 0.5 * piece - (2.0 * LN2) * merged[at : at + 1, :]


def call(kernel, outs, scratch=(), mib=24, **more):
    return pl.pallas_call(
        kernel,
        out_shape=outs,
        **more,
        scratch_shapes=list(scratch),
        compiler_params=pltpu.CompilerParams(vmem_limit_bytes=mib * 1024 * 1024),
    )


def shape(*dims, dtype=F32):
    return jax.ShapeDtypeStruct(dims, dtype)


def on_device(sources, log_source_mass, targets, log_target_mass, start_potential):
    near, far = ("y", "x"), ("z", "c")
    dims, own_rows = sources.shape
    own_cols = targets.shape[1]
    near_count, share_count = lax.axis_size(near), lax.axis_size("c")
    far_count = lax.axis_size(far)
    rows, cols = near_count * own_rows, share_count * own_cols
    row_tiles, col_tiles = rows // LANES, cols // LANES
    depth = len(LEFT) * ROWS

    def swap(value, axes):
        return lax.all_to_all(value, axes, 0, 0, tiled=True)

    src_send = pack((sources, log_source_mass[None]), shape(near_count, ROWS, LANES))
    src_all = swap(src_send, near)
    tgt_own = pack((targets, log_target_mass[None], start_potential[None]), shape(ROWS, own_cols))
    tgts = [tgt_own] + [
        lax.ppermute(tgt_own, "c", [(k, (k + shift) % share_count) for k in range(share_count)])
        for shift in range(1, share_count)
    ]
    tgt, tgt_mass, beta, top = call(
        functools.partial(target_kernel, dims, share_count),
        (
            shape(depth, cols, dtype=BF16),
            shape(col_tiles, LANES),
            shape(col_tiles, LANES),
            shape(1, LANES),
        ),
        [pltpu.VMEM((share_count, ROWS, own_cols), F32)],
    )(*tgts)
    row_send, src, src_mass, alpha, kept = call(
        functools.partial(first_kernel, dims),
        (
            shape(near_count, row_tiles, LANES),
            shape(depth, rows, dtype=BF16),
            shape(row_tiles, LANES),
            shape(row_tiles, LANES),
            shape(cols, rows),
        ),
        [pltpu.VMEM((row_tiles, LANES), F32)],
    )(src_all, tgt, top)
    column_scratch = [pltpu.VMEM((3 * ROWS, rows), BF16), pltpu.VMEM((col_tiles, LANES), F32)]
    row_all = swap(row_send, near)
    col_send = call(column_kernel, shape(far_count, col_tiles, LANES), column_scratch)(
        row_all, kept, src, src_mass, alpha, tgt, beta
    )
    col_all = swap(col_send, far)
    row_send = call(
        row_kernel,
        shape(near_count, row_tiles, LANES),
        [pltpu.VMEM((3 * ROWS, cols), BF16), pltpu.VMEM((row_tiles, LANES), F32)],
    )(col_all, kept, src, tgt, tgt_mass, beta, alpha)
    row_all = swap(row_send, near)
    col_send, merged = call(
        functools.partial(last_column_kernel, share_count),
        (shape(far_count, own_cols // LANES, LANES), shape(row_tiles, LANES)),
        column_scratch,
    )(row_all, kept, src, src_mass, alpha, tgt, beta)
    col_all = swap(col_send, far)
    row_potential, column_potential = call(
        functools.partial(final_kernel, near), (shape(1, own_rows), shape(own_cols // LANES, LANES))
    )(col_all, merged, sources, targets)
    return row_potential.reshape(own_rows), column_potential.reshape(own_cols)


def solution(mesh):
    split = Mesh(mesh.devices.reshape(8, 4, 4, 2), ("z", "y", "x", "c"))
    everywhere, column = ("z", "y", "x", "c"), ("y", "x", "c")
    return jax.shard_map(
        on_device,
        mesh=split,
        in_specs=(P(None, everywhere), P(everywhere), P(None, column), P(column), P(column)),
        out_specs=(P(everywhere), P(column)),
        check_vma=False,
    )
```
